32 devices in a mesh: row: 4 (over y, x), query: 8 (over z, core).
Axes of the slice: x: 2, y: 2, z: 4, core: 2. Of those that a mesh axis runs over, the one named last changes fastest.
Arguments:
- logits: float32 [512, 1024], P('row'), may hold values from -9 to 309
- attributes: int32 [3, 16384], P(None, 'query'), may hold values from 0 to 63
- values: int32 [3, 16384], P(None, 'query'), may hold values from 0 to 15
- targets: float32 [16384], P('query'), may hold values from 0.25 to 1.75
Outputs:
- new_rows: float32 [512, 1024], P('row')
- residual: float32 [16384], P('query')
The draws below stay inside these ranges and needn't reach their ends.
All inputs are finite; a program needn't handle non-finite values.
Results may differ from the reference program's by a relative error of at most 0.0064.
Values sent between devices are 32-bit elements; how exact they have to be, the bound alone decides.
A program may use at most 64 MiB of HBM per device.

```python
import jax
import jax.numpy as jnp
from jax import lax

ATTRS = 64
VALS = 16
QDEV = 2048
COLS = 1024
ROWS = 512
QUERIES = 16384
N_QUERY = 8


def draw_logits(key, part):
    base_key = jax.random.fold_in(jax.random.fold_in(key, 17), 0)
    base = jnp.clip(1.5 * jax.random.normal(base_key, (ROWS, ATTRS, VALS), jnp.float32), -9.0, 9.0)
    return base.reshape(ROWS, ATTRS * VALS)


def plant(values, own_key, least, high):
    index_at = [jax.random.randint(jax.random.fold_in(own_key, axis), (), 0, length) for axis, length in enumerate(values.shape)]
    longest = values.shape.index(max(values.shape))
    neighbour = index_at[:longest] + [(index_at[longest] + 1) % values.shape[longest]] + index_at[longest + 1:]
    return values.at[tuple(index_at)].set(least).at[tuple(neighbour)].set(high)


def levels(key, shape, shards, least, high):
    level = 1.0
    for dim, shards_of in shards:
        heights = jax.random.uniform(jax.random.fold_in(jax.random.fold_in(key, 6), dim), (shards_of,), jnp.float32, least / len(shards), high / len(shards))
        level = level * jnp.repeat(jnp.exp(heights), shape[dim] // shards_of).reshape((-1,) + (1,) * (len(shape) - 1 - dim))
    return level


def setup_inputs(seed: int = 0) -> dict:
    key_of = jax.random.split(jax.random.key(seed), 5)
    return {
        "logits": draw_logits(jax.random.fold_in(key_of[4], 71), 0),
        "attributes": plant(jax.random.randint(key_of[1], (3, QUERIES), 0, ATTRS), jax.random.fold_in(key_of[1], 1), 0, ATTRS - 1).astype(jnp.int32),
        "values": plant(jax.random.randint(key_of[2], (3, QUERIES), 0, VALS), jax.random.fold_in(key_of[2], 1), 0, VALS - 1).astype(jnp.int32),
        "targets": jnp.clip(0.25 + 1.5 * jax.random.uniform(key_of[3], (QUERIES,), jnp.float32) ** levels(key_of[3], (QUERIES,), ((0, 8),), -0.2, 0.2), 0.25, 1.75),
    }


STEP_RATE = 2.0


def group_softmax(logit_rows):
    row_count = logit_rows.shape[0]
    grouped = logit_rows.reshape(row_count, -1, VALS)
    return jax.nn.softmax(grouped, axis=-1).reshape(row_count, -1)


def relaxed_update(logit_rows, relaxed, accumulated):
    row_count = logit_rows.shape[0]
    scaled = float(VALS * VALS) * accumulated
    grouped_p = relaxed.reshape(row_count, -1, VALS)
    grouped_d = scaled.reshape(row_count, -1, VALS)
    weighted_mean = jnp.sum(grouped_p * grouped_d, axis=-1, keepdims=True)
    tangent = (grouped_p * (grouped_d - weighted_mean)).reshape(row_count, -1)
    return group_softmax(logit_rows - STEP_RATE * tangent)


def reference(logits, attributes, values, targets):
    total_rows = logits.shape[0]
    relaxed = group_softmax(logits)
    relaxed_b = relaxed.astype(jnp.bfloat16)
    columns = (attributes * VALS + values).astype(jnp.int32)
    blocks = columns.reshape(3, N_QUERY, QDEV).transpose(1, 0, 2)
    answer_scale = float(VALS ** 3) / total_rows

    def forward(query_block):
        pick_one = relaxed_b[:, query_block[0]].astype(jnp.float32)
        pick_two = relaxed_b[:, query_block[1]].astype(jnp.float32)
        pick_three = relaxed_b[:, query_block[2]].astype(jnp.float32)
        return jnp.sum(pick_one * pick_two * pick_three, axis=0)

    answers = lax.map(forward, blocks).reshape(-1) * answer_scale
    residual = answers - targets

    def backward(running, inputs):
        query_block, misfit = inputs
        pick_one = relaxed_b[:, query_block[0]].astype(jnp.float32)
        pick_two = relaxed_b[:, query_block[1]].astype(jnp.float32)
        pick_three = relaxed_b[:, query_block[2]].astype(jnp.float32)
        weights = ((pick_two * pick_three) * misfit[None, :],
                   (pick_one * pick_three) * misfit[None, :],
                   (pick_one * pick_two) * misfit[None, :])
        for position in range(3):
            rounded = weights[position].astype(jnp.bfloat16).astype(jnp.float32)
            running = running + jax.ops.segment_sum(rounded.T, query_block[position], num_segments=COLS)
        return running, None

    start_value = jnp.zeros((COLS, total_rows), jnp.float32)
    accum_t, unused = lax.scan(backward, start_value, (blocks, residual.reshape(N_QUERY, QDEV)))
    new_rows = relaxed_update(logits, relaxed, accum_t.T)
    return new_rows, residual
```

```python
import functools

import jax
import jax.numpy as jnp
from jax import lax
from jax.experimental import pallas as pl
from jax.experimental.pallas import tpu as pltpu
from jax.sharding import PartitionSpec as P

VALS = 16
STEP_RATE = 2.0
CHUNK = 256
BLOCK = 256
LANES = 128
MESH = pl.DeviceIdType.MESH


def group_softmax(tall):
    cols, rows = tall.shape
    grouped = tall.reshape(cols // VALS, VALS, rows)
    shifted = jnp.exp(grouped - jnp.max(grouped, axis=1, keepdims=True))
    return (shifted / jnp.sum(shifted, axis=1, keepdims=True)).reshape(cols, rows)


def kernel(
    n_row, n_query, total_rows,
    log_ref, attr_ref, val_ref, tgt_ref, new_ref, res_ref,
    log_t, rel_t, rel_b, sel, pair, wgt, ans, acc, sib, zin, gat,
    ans_send, ans_recv, sib_send, sib_recv, z_send, z_recv, ag_send, ag_recv, fw_send, fw_recv,
):
    me_r = lax.axis_index("row")
    me_q = lax.axis_index("query")
    me_z, core = me_q // 2, me_q % 2
    other = 1 - core
    n_z = n_query // 2
    rows, cols = log_ref.shape
    queries = attr_ref.shape[1]
    half_q = queries // 2
    half_c = cols // 2
    share = half_c // n_z
    per_block = BLOCK // share
    n_block = half_c // BLOCK
    sibling = (me_r, me_z * 2 + other)

    def remote(src, dst, ssem, rsem, device):
        return pltpu.make_async_remote_copy(
            src_ref=src, dst_ref=dst, send_sem=ssem, recv_sem=rsem,
            device_id=device, device_id_type=MESH,
        )

    barrier = pltpu.get_barrier_semaphore()
    for d in range(1, n_row):
        pl.semaphore_signal(barrier, inc=1, device_id=(lax.rem(me_r + d, n_row), me_q), device_id_type=MESH)
    for d in range(1, n_z):
        pl.semaphore_signal(
            barrier, inc=1, device_id=(me_r, lax.rem(me_z + d, n_z) * 2 + core), device_id_type=MESH
        )
    pl.semaphore_signal(barrier, inc=1, device_id=sibling, device_id_type=MESH)

    for b in range(cols // LANES):
        part = slice(b * LANES, (b + 1) * LANES)
        tall = log_ref[:, part].T
        log_t[part, :] = tall
        relaxed = group_softmax(tall)
        rel_t[part, :] = relaxed
        rel_b[:, part] = relaxed.T.astype(jnp.bfloat16)

    positions = lax.broadcasted_iota(jnp.int32, (cols, CHUNK), 0)
    chunks = half_q // CHUNK

    def ans_copy(h, dst_row, slot, d):
        return remote(ans.at[h, slot], ans.at[h, slot], ans_send.at[h, d], ans_recv.at[h, slot], (dst_row, me_q))

    for h in range(2):

        def forward(c, carry, h=h):
            at = pl.multiple_of(h * half_q + c * CHUNK, CHUNK)
            base = pl.multiple_of(at * 3, CHUNK)
            picked = []
            for k in range(3):
                column = attr_ref[k : k + 1, pl.ds(at, CHUNK)] * VALS + val_ref[k : k + 1, pl.ds(at, CHUNK)]
                one_hot = (positions == column).astype(jnp.float32).astype(jnp.bfloat16)
                sel[:, pl.ds(base + k * CHUNK, CHUNK)] = one_hot
                picked.append(jnp.dot(rel_b[...], one_hot, preferred_element_type=jnp.float32))
            first = picked[0] * picked[1]
            pair[:, pl.ds(base, CHUNK)] = picked[1] * picked[2]
            pair[:, pl.ds(base + CHUNK, CHUNK)] = picked[0] * picked[2]
            pair[:, pl.ds(base + 2 * CHUNK, CHUNK)] = first
            partial = jnp.sum(first * picked[2], axis=0, keepdims=True)
            for i in range(CHUNK // LANES):
                ans[h, me_r, pl.ds(c * (CHUNK // LANES) + i, 1), :] = partial[:, i * LANES : (i + 1) * LANES]
            return carry

        lax.fori_loop(0, chunks, forward, 0)
        if h == 0:
            pl.semaphore_wait(barrier, n_row - 1 + n_z)
        for d in range(1, n_row):
            ans_copy(h, lax.rem(me_r + d, n_row), me_r, d).start()

    answer_scale = float(VALS**3) / total_rows
    half_lines = half_q // LANES

    def rows_at(block):
        return pl.ds(pl.multiple_of(block * BLOCK, BLOCK), BLOCK)

    def sums(block, h):
        span = slice(h * 3 * half_q, (h + 1) * 3 * half_q)
        return lax.dot_general(
            sel[rows_at(block), span], wgt[:, span], (((1,), (1,)), ((), ())),
            preferred_element_type=jnp.float32,
        )

    def piece(side, z):
        return pl.ds(pl.multiple_of(side * half_c + z * share, share), share)

    def sib_copy(side, z):
        return remote(acc.at[piece(side, z)], sib.at[z], sib_send.at[z], sib_recv.at[z], sibling)

    def z_copy(dst_z, slot):
        return remote(
            acc.at[piece(core, dst_z)], zin.at[slot], z_send.at[dst_z], z_recv.at[slot], (me_r, dst_z * 2 + core)
        )

    for h in range(2):
        for d in range(1, n_row):
            ans_copy(h, me_r, lax.rem(me_r + n_row - d, n_row), d).wait_recv()
        total = ans[h, 0]
        for r in range(1, n_row):
            total = total + ans[h, r]
        lines = slice(h * half_lines, (h + 1) * half_lines)
        residual = total * answer_scale - tgt_ref[lines, :]
        res_ref[lines, :] = residual
        for line in range(half_lines):
            chunk, inner = divmod(line * LANES, CHUNK)
            for k in range(3):
                start = h * 3 * half_q + (chunk * 3 + k) * CHUNK + inner
                span = slice(start, start + LANES)
                wgt[:, span] = (pair[:, span] * residual[line : line + 1, :]).astype(jnp.bfloat16)
        if h == 0:
            for block in range(2 * n_block):
                acc[rows_at(block), :] = sums(block, 0)
    for b in range(n_block):
        block = other * n_block + b
        acc[rows_at(block), :] += sums(block, 1)
        for i in range(per_block):
            sib_copy(other, b * per_block + i).start()
    for b in range(n_block):
        inner = lax.rem(me_z // per_block + 1 + b, n_block)
        block = core * n_block + inner
        acc[rows_at(block), :] += sums(block, 1)
        for i in range(per_block):
            z = inner * per_block + i
            sib_copy(core, z).wait_recv()
            summed = acc[piece(core, z), :] + sib[z]

            @pl.when(z != me_z)
            def _():
                acc[piece(core, z), :] = summed
                z_copy(z, me_z).start()

            @pl.when(z == me_z)
            def _():
                zin[me_z] = summed

    mine = piece(core, me_z)
    logit_share, relaxed_share = log_t[mine, :], rel_t[mine, :]
    for d in range(1, n_z):
        z_copy(me_z, lax.rem(me_z + d, n_z)).wait_recv()
    accumulated = zin[0]
    for z in range(1, n_z):
        accumulated = accumulated + zin[z]
    grouped_d = (float(VALS * VALS) * accumulated).reshape(share // VALS, VALS, rows)
    grouped_p = relaxed_share.reshape(share // VALS, VALS, rows)
    weighted_mean = jnp.sum(grouped_p * grouped_d, axis=1, keepdims=True)
    tangent = (grouped_p * (grouped_d - weighted_mean)).reshape(share, rows)
    gat[mine, :] = group_softmax(logit_share - STEP_RATE * tangent)

    def ag_copy(dst_z, z):
        return remote(
            gat.at[piece(core, z)], gat.at[piece(core, z)], ag_send.at[dst_z], ag_recv.at[z], (me_r, dst_z * 2 + core)
        )

    def fw_copy(side, z):
        return remote(gat.at[piece(side, z)], gat.at[piece(side, z)], fw_send.at[z], fw_recv.at[z], sibling)

    for d in range(1, n_z):
        ag_copy(lax.rem(me_z + d, n_z), me_z).start()
    fw_copy(core, me_z).start()
    for d in range(1, n_z):
        z = lax.rem(me_z + d, n_z)
        ag_copy(z, z).wait_recv()
        fw_copy(core, z).start()
    for d in range(n_z):
        fw_copy(other, lax.rem(me_z + d, n_z)).wait_recv()
    for b in range(cols // LANES):
        part = slice(b * LANES, (b + 1) * LANES)
        new_ref[:, part] = gat[part, :].T

    for h in range(2):
        for d in range(1, n_row):
            ans_copy(h, lax.rem(me_r + d, n_row), me_r, d).wait_send()
    for z in range(n_z):
        sib_copy(other, z).wait_send()
    for d in range(1, n_z):
        z = lax.rem(me_z + d, n_z)
        z_copy(z, me_z).wait_send()
        ag_copy(z, me_z).wait_send()
    for z in range(n_z):
        fw_copy(core, z).wait_send()


def local(n_row, n_query, logits, attributes, values, targets):
    rows, cols = logits.shape
    queries = attributes.shape[1]
    n_z = n_query // 2
    share = cols // n_query
    dma = pltpu.SemaphoreType.DMA
    vmem = pl.BlockSpec(memory_space=pltpu.VMEM)
    new_rows, residual = pl.pallas_call(
        functools.partial(kernel, n_row, n_query, rows * n_row),
        out_shape=(
            jax.ShapeDtypeStruct((rows, cols), jnp.float32),
            jax.ShapeDtypeStruct((queries // LANES, LANES), jnp.float32),
        ),
        in_specs=[vmem] * 4,
        out_specs=(vmem, vmem),
        scratch_shapes=[
            pltpu.VMEM((cols, rows), jnp.float32),
            pltpu.VMEM((cols, rows), jnp.float32),
            pltpu.VMEM((rows, cols), jnp.bfloat16),
            pltpu.VMEM((cols, 3 * queries), jnp.bfloat16),
            pltpu.VMEM((rows, 3 * queries), jnp.float32),
            pltpu.VMEM((rows, 3 * queries), jnp.bfloat16),
            pltpu.VMEM((2, n_row, queries // 2 // LANES, LANES), jnp.float32),
            pltpu.VMEM((cols, rows), jnp.float32),
            pltpu.VMEM((n_z, share, rows), jnp.float32),
            pltpu.VMEM((n_z, share, rows), jnp.float32),
            pltpu.VMEM((cols, rows), jnp.float32),
            dma((2, n_row)), dma((2, n_row)),
            dma((n_z,)), dma((n_z,)), dma((n_z,)), dma((n_z,)),
            dma((n_z,)), dma((n_z,)), dma((n_z,)), dma((n_z,)),
        ],
        compiler_params=pltpu.CompilerParams(
            collective_id=0, has_side_effects=True, vmem_limit_bytes=48 * 1024 * 1024
        ),
    )(logits, attributes, values, targets.reshape(queries // LANES, LANES))
    return new_rows, residual.reshape(queries)


def solution(mesh):
    placed = (P("row", None), P(None, "query"), P(None, "query"), P("query"))
    return jax.shard_map(
        functools.partial(local, mesh.shape["row"], mesh.shape["query"]),
        mesh=mesh, in_specs=placed, out_specs=(P("row", None), P("query")), check_vma=False,
    )
```

```python
import functools

import jax
import jax.numpy as jnp
from jax import lax
from jax.experimental import pallas as pl
from jax.experimental.pallas import tpu as pltpu
from jax.sharding import PartitionSpec as P

VALS = 16
STEP_RATE = 2.0
CHUNK = 256
BLOCK = 256
LANES = 128
MESH = pl.DeviceIdType.MESH


def group_softmax(tall):
    cols, rows = tall.shape
    grouped = tall.reshape(cols // VALS, VALS, rows)
    shifted = jnp.exp(grouped - jnp.max(grouped, axis=1, keepdims=True))
    return (shifted / jnp.sum(shifted, axis=1, keepdims=True)).reshape(cols, rows)


def kernel(
    n_row, n_query, total_rows,
    log_ref, meta_ref, gat, res_ref,
    tgt_ref, log_t, rel_t, rel_b, sel, pair, wgt, ans, acc, sib, zin,
    ans_send, ans_recv, sib_send, sib_recv, z_send, z_recv, ag_send, ag_recv, fw_send, fw_recv,
):
    me_r = lax.axis_index("row")
    me_q = lax.axis_index("query")
    me_z, core = me_q // 2, me_q % 2
    other = 1 - core
    n_z = n_query // 2
    rows, cols = log_ref.shape
    queries = meta_ref.shape[1]
    half_q = queries // 2
    half_c = cols // 2
    share = half_c // n_z
    per_block = BLOCK // share
    n_block = half_c // BLOCK
    sibling = (me_r, me_z * 2 + other)

    def remote(src, dst, ssem, rsem, device):
        return pltpu.make_async_remote_copy(
            src_ref=src, dst_ref=dst, send_sem=ssem, recv_sem=rsem,
            device_id=device, device_id_type=MESH,
        )

    barrier = pltpu.get_barrier_semaphore()
    for d in range(1, n_row):
        pl.semaphore_signal(barrier, inc=1, device_id=(lax.rem(me_r + d, n_row), me_q), device_id_type=MESH)
    for d in range(1, n_z):
        pl.semaphore_signal(
            barrier, inc=1, device_id=(me_r, lax.rem(me_z + d, n_z) * 2 + core), device_id_type=MESH
        )
    pl.semaphore_signal(barrier, inc=1, device_id=sibling, device_id_type=MESH)

    for b in range(cols // LANES):
        part = slice(b * LANES, (b + 1) * LANES)
        tall = log_ref[:, part].T
        log_t[part, :] = tall
        relaxed = group_softmax(tall)
        rel_t[part, :] = relaxed
        rel_b[:, part] = relaxed.T.astype(jnp.bfloat16)

    for line in range(queries // LANES):
        tgt_ref[line : line + 1, :] = meta_ref[3:4, line * LANES : (line + 1) * LANES]
    positions = lax.broadcasted_iota(jnp.int32, (cols, CHUNK), 0).astype(jnp.float32)
    chunks = half_q // CHUNK

    def ans_copy(h, dst_row, slot, d):
        return remote(ans.at[h, slot], ans.at[h, slot], ans_send.at[h, d], ans_recv.at[h, slot], (dst_row, me_q))

    for h in range(2):

        def forward(c, carry, h=h):
            at = pl.multiple_of(h * half_q + c * CHUNK, CHUNK)
            base = pl.multiple_of(at * 3, CHUNK)
            picked = []
            for k in range(3):
                column = meta_ref[k : k + 1, pl.ds(at, CHUNK)]
                one_hot = (positions == column).astype(jnp.float32).astype(jnp.bfloat16)
                sel[:, pl.ds(base + k * CHUNK, CHUNK)] = one_hot
                picked.append(jnp.dot(rel_b[...], one_hot, preferred_element_type=jnp.float32))
            first = picked[0] * picked[1]
            pair[:, pl.ds(base, CHUNK)] = picked[1] * picked[2]
            pair[:, pl.ds(base + CHUNK, CHUNK)] = picked[0] * picked[2]
            pair[:, pl.ds(base + 2 * CHUNK, CHUNK)] = first
            partial = jnp.sum(first * picked[2], axis=0, keepdims=True)
            for i in range(CHUNK // LANES):
                ans[h, me_r, pl.ds(c * (CHUNK // LANES) + i, 1), :] = partial[:, i * LANES : (i + 1) * LANES]
            return carry

        lax.fori_loop(0, chunks, forward, 0)
        if h == 0:
            pl.semaphore_wait(barrier, n_row - 1 + n_z)
        for d in range(1, n_row):
            ans_copy(h, lax.rem(me_r + d, n_row), me_r, d).start()

    answer_scale = float(VALS**3) / total_rows
    half_lines = half_q // LANES

    def rows_at(block):
        return pl.ds(pl.multiple_of(block * BLOCK, BLOCK), BLOCK)

    def sums(block, h):
        span = slice(h * 3 * half_q, (h + 1) * 3 * half_q)
        return lax.dot_general(
            sel[rows_at(block), span], wgt[:, span], (((1,), (1,)), ((), ())),
            preferred_element_type=jnp.float32,
        )

    def piece(side, z):
        return pl.ds(pl.multiple_of(side * half_c + z * share, share), share)

    def sib_copy(side, z):
        return remote(acc.at[piece(side, z)], sib.at[z], sib_send.at[z], sib_recv.at[z], sibling)

    def z_copy(dst_z, slot):
        return remote(
            acc.at[piece(core, dst_z)], zin.at[slot], z_send.at[dst_z], z_recv.at[slot], (me_r, dst_z * 2 + core)
        )

    for h in range(2):
        for d in range(1, n_row):
            ans_copy(h, me_r, lax.rem(me_r + n_row - d, n_row), d).wait_recv()
        total = ans[h, 0]
        for r in range(1, n_row):
            total = total + ans[h, r]
        lines = slice(h * half_lines, (h + 1) * half_lines)
        residual = total * answer_scale - tgt_ref[lines, :]
        res_ref[lines, :] = residual
        for line in range(half_lines):
            chunk, inner = divmod(line * LANES, CHUNK)
            for k in range(3):
                start = h * 3 * half_q + (chunk * 3 + k) * CHUNK + inner
                span = slice(start, start + LANES)
                wgt[:, span] = (pair[:, span] * residual[line : line + 1, :]).astype(jnp.bfloat16)
        if h == 0:
            for block in range(2 * n_block):
                acc[rows_at(block), :] = sums(block, 0)
    for b in range(n_block):
        block = other * n_block + b
        acc[rows_at(block), :] += sums(block, 1)
        for i in range(per_block):
            sib_copy(other, b * per_block + i).start()
    for b in range(n_block):
        inner = lax.rem(me_z // per_block + 1 + b, n_block)
        block = core * n_block + inner
        acc[rows_at(block), :] += sums(block, 1)
        for i in range(per_block):
            z = inner * per_block + i
            sib_copy(core, z).wait_recv()
            summed = acc[piece(core, z), :] + sib[z]

            @pl.when(z != me_z)
            def _():
                acc[piece(core, z), :] = summed
                z_copy(z, me_z).start()

            @pl.when(z == me_z)
            def _():
                zin[me_z] = summed

    mine = piece(core, me_z)
    logit_share, relaxed_share = log_t[mine, :], rel_t[mine, :]
    for d in range(1, n_z):
        z_copy(me_z, lax.rem(me_z + d, n_z)).wait_recv()
    accumulated = zin[0]
    for z in range(1, n_z):
        accumulated = accumulated + zin[z]
    grouped_d = (float(VALS * VALS) * accumulated).reshape(share // VALS, VALS, rows)
    grouped_p = relaxed_share.reshape(share // VALS, VALS, rows)
    weighted_mean = jnp.sum(grouped_p * grouped_d, axis=1, keepdims=True)
    tangent = (grouped_p * (grouped_d - weighted_mean)).reshape(share, rows)
    gat[mine, :] = group_softmax(logit_share - STEP_RATE * tangent)

    def ag_copy(dst_z, z):
        return remote(
            gat.at[piece(core, z)], gat.at[piece(core, z)], ag_send.at[dst_z], ag_recv.at[z], (me_r, dst_z * 2 + core)
        )

    def fw_copy(side, z):
        return remote(gat.at[piece(side, z)], gat.at[piece(side, z)], fw_send.at[z], fw_recv.at[z], sibling)

    for d in range(1, n_z):
        ag_copy(lax.rem(me_z + d, n_z), me_z).start()
    fw_copy(core, me_z).start()
    for d in range(1, n_z):
        z = lax.rem(me_z + d, n_z)
        ag_copy(z, z).wait_recv()
        fw_copy(core, z).start()
    for d in range(n_z):
        fw_copy(other, lax.rem(me_z + d, n_z)).wait_recv()
    for h in range(2):
        for d in range(1, n_row):
            ans_copy(h, lax.rem(me_r + d, n_row), me_r, d).wait_send()
    for z in range(n_z):
        sib_copy(other, z).wait_send()
    for d in range(1, n_z):
        z = lax.rem(me_z + d, n_z)
        z_copy(z, me_z).wait_send()
        ag_copy(z, me_z).wait_send()
    for z in range(n_z):
        fw_copy(core, z).wait_send()


def finish(tall_ref, misfit_ref, new_ref, res_ref):
    for b in range(tall_ref.shape[0] // LANES):
        part = slice(b * LANES, (b + 1) * LANES)
        new_ref[:, part] = tall_ref[part, :].T
    res_ref[...] = misfit_ref[...]


def local(n_row, n_query, logits, attributes, values, targets):
    rows, cols = logits.shape
    queries = attributes.shape[1]
    n_z = n_query // 2
    share = cols // n_query
    dma = pltpu.SemaphoreType.DMA
    vmem = pl.BlockSpec(memory_space=pltpu.VMEM)
    columns = (attributes * VALS + values).astype(jnp.float32)
    meta = jnp.concatenate([columns, targets[None, :]], axis=0)
    tall, misfit = pl.pallas_call(
        functools.partial(kernel, n_row, n_query, rows * n_row),
        out_shape=(
            jax.ShapeDtypeStruct((cols, rows), jnp.float32),
            jax.ShapeDtypeStruct((queries // LANES, LANES), jnp.float32),
        ),
        in_specs=[vmem] * 2,
        out_specs=(vmem, vmem),
        scratch_shapes=[
            pltpu.VMEM((queries // LANES, LANES), jnp.float32),
            pltpu.VMEM((cols, rows), jnp.float32),
            pltpu.VMEM((cols, rows), jnp.float32),
            pltpu.VMEM((rows, cols), jnp.bfloat16),
            pltpu.VMEM((cols, 3 * queries), jnp.bfloat16),
            pltpu.VMEM((rows, 3 * queries), jnp.float32),
            pltpu.VMEM((rows, 3 * queries), jnp.bfloat16),
            pltpu.VMEM((2, n_row, queries // 2 // LANES, LANES), jnp.float32),
            pltpu.VMEM((cols, rows), jnp.float32),
            pltpu.VMEM((n_z, share, rows), jnp.float32),
            pltpu.VMEM((n_z, share, rows), jnp.float32),
            dma((2, n_row)), dma((2, n_row)),
            dma((n_z,)), dma((n_z,)), dma((n_z,)), dma((n_z,)),
            dma((n_z,)), dma((n_z,)), dma((n_z,)), dma((n_z,)),
        ],
        compiler_params=pltpu.CompilerParams(
            collective_id=0, has_side_effects=True, vmem_limit_bytes=48 * 1024 * 1024
        ),
    )(logits, meta)
    new_rows, residual = pl.pallas_call(
        finish,
        out_shape=(
            jax.ShapeDtypeStruct((rows, cols), jnp.float32),
            jax.ShapeDtypeStruct((queries // LANES, LANES), jnp.float32),
        ),
        in_specs=[vmem, vmem],
        out_specs=(vmem, vmem),
        compiler_params=pltpu.CompilerParams(vmem_limit_bytes=4 * 1024 * 1024),
    )(tall, misfit)
    return new_rows, residual.reshape(queries)


def solution(mesh):
    placed = (P("row", None), P(None, "query"), P(None, "query"), P("query"))
    return jax.shard_map(
        functools.partial(local, mesh.shape["row"], mesh.shape["query"]),
        mesh=mesh, in_specs=placed, out_specs=(P("row", None), P("query")), check_vma=False,
    )
```

```python
import functools

import jax
import jax.numpy as jnp
from jax import lax
from jax.experimental import pallas as pl
from jax.experimental.pallas import tpu as pltpu
from jax.sharding import PartitionSpec as P

VALS = 16
STEP_RATE = 2.0
CHUNK = 256
BLOCK = 256
LANES = 128
MESH = pl.DeviceIdType.MESH


def group_softmax(tall):
    cols, rows = tall.shape
    grouped = tall.reshape(cols // VALS, VALS, rows)
    shifted = jnp.exp(grouped - jnp.max(grouped, axis=1, keepdims=True))
    return (shifted / jnp.sum(shifted, axis=1, keepdims=True)).reshape(cols, rows)


def kernel(
    n_row, n_query, total_rows,
    log_ref, meta_ref, gat, res_ref,
    tgt_ref, log_t, rel_t, rel_b, sel, pair, wgt, ans, acc, sib, zin,
    ans_send, ans_recv, sib_send, sib_recv, z_send, z_recv, ag_send, ag_recv, fw_send, fw_recv,
):
    me_r = lax.axis_index("row")
    me_q = lax.axis_index("query")
    me_z, core = me_q // 2, me_q % 2
    other = 1 - core
    n_z = n_query // 2
    rows, cols = log_ref.shape
    queries = meta_ref.shape[1]
    half_q = queries // 2
    half_c = cols // 2
    share = half_c // n_z
    per_block = BLOCK // share
    n_block = half_c // BLOCK
    sibling = (me_r, me_z * 2 + other)

    def remote(src, dst, ssem, rsem, device):
        return pltpu.make_async_remote_copy(
            src_ref=src, dst_ref=dst, send_sem=ssem, recv_sem=rsem,
            device_id=device, device_id_type=MESH,
        )

    barrier = pltpu.get_barrier_semaphore()
    for d in range(1, n_row):
        pl.semaphore_signal(barrier, inc=1, device_id=(lax.rem(me_r + d, n_row), me_q), device_id_type=MESH)
    for d in range(1, n_z):
        pl.semaphore_signal(
            barrier, inc=1, device_id=(me_r, lax.rem(me_z + d, n_z) * 2 + core), device_id_type=MESH
        )
    pl.semaphore_signal(barrier, inc=1, device_id=sibling, device_id_type=MESH)

    for b in range(cols // LANES):
        part = slice(b * LANES, (b + 1) * LANES)
        tall = log_ref[:, part].T
        log_t[part, :] = tall
        relaxed = group_softmax(tall)
        rel_t[part, :] = relaxed
        rel_b[:, part] = relaxed.T.astype(jnp.bfloat16)

    for line in range(queries // LANES):
        tgt_ref[line : line + 1, :] = meta_ref[3:4, line * LANES : (line + 1) * LANES]
    positions = lax.broadcasted_iota(jnp.int32, (cols, CHUNK), 0).astype(jnp.float32)
    chunks = half_q // CHUNK

    def ans_copy(h, dst_row, slot, d):
        return remote(ans.at[h, slot], ans.at[h, slot], ans_send.at[h, d], ans_recv.at[h, slot], (dst_row, me_q))

    for h in range(2):

        def forward(c, carry, h=h):
            at = pl.multiple_of(h * half_q + c * CHUNK, CHUNK)
            base = pl.multiple_of(at * 3, CHUNK)
            picked = []
            for k in range(3):
                column = meta_ref[k : k + 1, pl.ds(at, CHUNK)]
                one_hot = (positions == column).astype(jnp.float32).astype(jnp.bfloat16)
                sel[:, pl.ds(base + k * CHUNK, CHUNK)] = one_hot
                picked.append(jnp.dot(rel_b[...], one_hot, preferred_element_type=jnp.float32))
            first = picked[0] * picked[1]
            pair[:, pl.ds(base, CHUNK)] = picked[1] * picked[2]
            pair[:, pl.ds(base + CHUNK, CHUNK)] = picked[0] * picked[2]
            pair[:, pl.ds(base + 2 * CHUNK, CHUNK)] = first
            partial = jnp.sum(first * picked[2], axis=0, keepdims=True)
            for i in range(CHUNK // LANES):
                ans[h, me_r, pl.ds(c * (CHUNK // LANES) + i, 1), :] = partial[:, i * LANES : (i + 1) * LANES]
            return carry

        lax.fori_loop(0, chunks, forward, 0)
        if h == 0:
            pl.semaphore_wait(barrier, n_row - 1 + n_z)
        for d in range(1, n_row):
            ans_copy(h, lax.rem(me_r + d, n_row), me_r, d).start()

    answer_scale = float(VALS**3) / total_rows
    half_lines = half_q // LANES

    def rows_at(block):
        return pl.ds(pl.multiple_of(block * BLOCK, BLOCK), BLOCK)

    def sums(block, h):
        span = slice(h * 3 * half_q, (h + 1) * 3 * half_q)
        return lax.dot_general(
            sel[rows_at(block), span], wgt[:, span], (((1,), (1,)), ((), ())),
            preferred_element_type=jnp.float32,
        )

    def piece(side, z):
        return pl.ds(pl.multiple_of(side * half_c + z * share, share), share)

    def sib_copy(side, z):
        return remote(acc.at[piece(side, z)], sib.at[z], sib_send.at[z], sib_recv.at[z], sibling)

    def z_copy(dst_z, slot):
        return remote(
            acc.at[piece(core, dst_z)], zin.at[slot], z_send.at[dst_z], z_recv.at[slot], (me_r, dst_z * 2 + core)
        )

    lower = me_z < n_z // 2

    def inner_at(b):
        return jnp.where(lower, n_block - 1 - b, b)

    def piece_at(b, i):
        return inner_at(b) * per_block + jnp.where(lower, per_block - 1 - i, i)

    for h in range(2):
        for d in range(1, n_row):
            ans_copy(h, me_r, lax.rem(me_r + n_row - d, n_row), d).wait_recv()
        total = ans[h, 0]
        for r in range(1, n_row):
            total = total + ans[h, r]
        lines = slice(h * half_lines, (h + 1) * half_lines)
        residual = total * answer_scale - tgt_ref[lines, :]
        res_ref[lines, :] = residual
        for line in range(half_lines):
            chunk, inner = divmod(line * LANES, CHUNK)
            for k in range(3):
                start = h * 3 * half_q + (chunk * 3 + k) * CHUNK + inner
                span = slice(start, start + LANES)
                wgt[:, span] = (pair[:, span] * residual[line : line + 1, :]).astype(jnp.bfloat16)
        if h == 0:
            for block in range(2 * n_block):
                acc[rows_at(block), :] = sums(block, 0)
    for b in range(n_block):
        block = other * n_block + inner_at(b)
        acc[rows_at(block), :] += sums(block, 1)
        for i in range(per_block):
            sib_copy(other, piece_at(b, i)).start()
    for b in range(n_block):
        block = core * n_block + inner_at(b)
        acc[rows_at(block), :] += sums(block, 1)
        for i in range(per_block):
            z = piece_at(b, i)
            sib_copy(core, z).wait_recv()
            summed = acc[piece(core, z), :] + sib[z]

            @pl.when(z != me_z)
            def _():
                acc[piece(core, z), :] = summed
                z_copy(z, me_z).start()

            @pl.when(z == me_z)
            def _():
                zin[me_z] = summed

    mine = piece(core, me_z)
    logit_share, relaxed_share = log_t[mine, :], rel_t[mine, :]
    for d in range(1, n_z):
        z_copy(me_z, lax.rem(me_z + d, n_z)).wait_recv()
    accumulated = zin[0]
    for z in range(1, n_z):
        accumulated = accumulated + zin[z]
    grouped_d = (float(VALS * VALS) * accumulated).reshape(share // VALS, VALS, rows)
    grouped_p = relaxed_share.reshape(share // VALS, VALS, rows)
    weighted_mean = jnp.sum(grouped_p * grouped_d, axis=1, keepdims=True)
    tangent = (grouped_p * (grouped_d - weighted_mean)).reshape(share, rows)
    gat[mine, :] = group_softmax(logit_share - STEP_RATE * tangent)

    def toward(d):
        sign = jnp.where(me_z < n_z // 2, 1, n_z - 1)
        return lax.rem(me_z + sign * d, n_z)

    def ag_copy(dst_z, z):
        return remote(
            gat.at[piece(core, z)], gat.at[piece(core, z)], ag_send.at[dst_z], ag_recv.at[z], (me_r, dst_z * 2 + core)
        )

    def fw_copy(side, z):
        return remote(gat.at[piece(side, z)], gat.at[piece(side, z)], fw_send.at[z], fw_recv.at[z], sibling)

    for d in range(n_z - 1, 0, -1):
        ag_copy(toward(d), me_z).start()
    fw_copy(core, me_z).start()
    for d in range(1, n_z):
        z = toward(d)
        ag_copy(z, z).wait_recv()
        fw_copy(core, z).start()
    for d in range(n_z):
        fw_copy(other, toward(d)).wait_recv()
    for h in range(2):
        for d in range(1, n_row):
            ans_copy(h, lax.rem(me_r + d, n_row), me_r, d).wait_send()
    for z in range(n_z):
        sib_copy(other, z).wait_send()
    for d in range(1, n_z):
        z = lax.rem(me_z + d, n_z)
        z_copy(z, me_z).wait_send()
        ag_copy(z, me_z).wait_send()
    for z in range(n_z):
        fw_copy(core, z).wait_send()


def finish(tall_ref, misfit_ref, new_ref, res_ref):
    for b in range(tall_ref.shape[0] // LANES):
        part = slice(b * LANES, (b + 1) * LANES)
        new_ref[:, part] = tall_ref[part, :].T
    res_ref[...] = misfit_ref[...]


def local(n_row, n_query, logits, attributes, values, targets):
    rows, cols = logits.shape
    queries = attributes.shape[1]
    n_z = n_query // 2
    share = cols // n_query
    dma = pltpu.SemaphoreType.DMA
    vmem = pl.BlockSpec(memory_space=pltpu.VMEM)
    columns = (attributes * VALS + values).astype(jnp.float32)
    meta = jnp.concatenate([columns, targets[None, :]], axis=0)
    tall, misfit = pl.pallas_call(
        functools.partial(kernel, n_row, n_query, rows * n_row),
        out_shape=(
            jax.ShapeDtypeStruct((cols, rows), jnp.float32),
            jax.ShapeDtypeStruct((queries // LANES, LANES), jnp.float32),
        ),
        in_specs=[vmem] * 2,
        out_specs=(vmem, vmem),
        scratch_shapes=[
            pltpu.VMEM((queries // LANES, LANES), jnp.float32),
            pltpu.VMEM((cols, rows), jnp.float32),
            pltpu.VMEM((cols, rows), jnp.float32),
            pltpu.VMEM((rows, cols), jnp.bfloat16),
            pltpu.VMEM((cols, 3 * queries), jnp.bfloat16),
            pltpu.VMEM((rows, 3 * queries), jnp.float32),
            pltpu.VMEM((rows, 3 * queries), jnp.bfloat16),
            pltpu.VMEM((2, n_row, queries // 2 // LANES, LANES), jnp.float32),
            pltpu.VMEM((cols, rows), jnp.float32),
            pltpu.VMEM((n_z, share, rows), jnp.float32),
            pltpu.VMEM((n_z, share, rows), jnp.float32),
            dma((2, n_row)), dma((2, n_row)),
            dma((n_z,)), dma((n_z,)), dma((n_z,)), dma((n_z,)),
            dma((n_z,)), dma((n_z,)), dma((n_z,)), dma((n_z,)),
        ],
        compiler_params=pltpu.CompilerParams(
            collective_id=0, has_side_effects=True, vmem_limit_bytes=48 * 1024 * 1024
        ),
    )(logits, meta)
    new_rows, residual = pl.pallas_call(
        finish,
        out_shape=(
            jax.ShapeDtypeStruct((rows, cols), jnp.float32),
            jax.ShapeDtypeStruct((queries // LANES, LANES), jnp.float32),
        ),
        in_specs=[vmem, vmem],
        out_specs=(vmem, vmem),
        compiler_params=pltpu.CompilerParams(vmem_limit_bytes=4 * 1024 * 1024),
    )(tall, misfit)
    return new_rows, residual.reshape(queries)


def solution(mesh):
    placed = (P("row", None), P(None, "query"), P(None, "query"), P("query"))
    return jax.shard_map(
        functools.partial(local, mesh.shape["row"], mesh.shape["query"]),
        mesh=mesh, in_specs=placed, out_specs=(P("row", None), P("query")), check_vma=False,
    )
```

```python
import functools

import jax
import jax.numpy as jnp
from jax import lax
from jax.experimental import pallas as pl
from jax.experimental.pallas import tpu as pltpu
from jax.sharding import PartitionSpec as P

VALS = 16
STEP_RATE = 2.0
CHUNK = 256
BLOCK = 256
LANES = 128
MESH = pl.DeviceIdType.MESH


def group_softmax(tall):
    cols, rows = tall.shape
    grouped = tall.reshape(cols // VALS, VALS, rows)
    shifted = jnp.exp(grouped - jnp.max(grouped, axis=1, keepdims=True))
    return (shifted / jnp.sum(shifted, axis=1, keepdims=True)).reshape(cols, rows)


def kernel(
    n_row, n_query, total_rows,
    log_ref, meta_ref, gat, res_ref,
    tgt_ref, log_t, rel_t, rel_b, sel, pair, wgt, ans, acc, sib, zin,
    ans_send, ans_recv, sib_send, sib_recv, z_send, z_recv, ag_send, ag_recv, fw_send, fw_recv,
):
    me_r = lax.axis_index("row")
    me_q = lax.axis_index("query")
    me_z, core = me_q // 2, me_q % 2
    other = 1 - core
    n_z = n_query // 2
    rows, cols = log_ref.shape
    queries = meta_ref.shape[1]
    half_q = queries // 2
    half_c = cols // 2
    share = half_c // n_z
    per_block = BLOCK // share
    n_block = half_c // BLOCK
    sibling = (me_r, me_z * 2 + other)

    def remote(src, dst, ssem, rsem, device):
        return pltpu.make_async_remote_copy(
            src_ref=src, dst_ref=dst, send_sem=ssem, recv_sem=rsem,
            device_id=device, device_id_type=MESH,
        )

    barrier = pltpu.get_barrier_semaphore()
    for d in range(1, n_row):
        pl.semaphore_signal(barrier, inc=1, device_id=(lax.rem(me_r + d, n_row), me_q), device_id_type=MESH)
    for d in range(1, n_z):
        pl.semaphore_signal(
            barrier, inc=1, device_id=(me_r, lax.rem(me_z + d, n_z) * 2 + core), device_id_type=MESH
        )
    pl.semaphore_signal(barrier, inc=1, device_id=sibling, device_id_type=MESH)

    for b in range(cols // LANES):
        part = slice(b * LANES, (b + 1) * LANES)
        tall = log_ref[:, part].T
        log_t[part, :] = tall
        relaxed = group_softmax(tall)
        rel_t[part, :] = relaxed
        rel_b[:, part] = relaxed.T.astype(jnp.bfloat16)

    for line in range(queries // LANES):
        tgt_ref[line : line + 1, :] = meta_ref[3:4, line * LANES : (line + 1) * LANES]
    positions = lax.broadcasted_iota(jnp.int32, (cols, CHUNK), 0).astype(jnp.float32)
    chunks = half_q // CHUNK

    def ans_copy(h, dst_row, slot, d):
        return remote(ans.at[h, slot], ans.at[h, slot], ans_send.at[h, d], ans_recv.at[h, slot], (dst_row, me_q))

    for h in range(2):

        def forward(c, carry, h=h):
            at = pl.multiple_of(h * half_q + c * CHUNK, CHUNK)
            base = pl.multiple_of(at * 3, CHUNK)
            picked = []
            for k in range(3):
                column = meta_ref[k : k + 1, pl.ds(at, CHUNK)]
                one_hot = (positions == column).astype(jnp.float32).astype(jnp.bfloat16)
                sel[:, pl.ds(base + k * CHUNK, CHUNK)] = one_hot
                picked.append(jnp.dot(rel_b[...], one_hot, preferred_element_type=jnp.float32))
            first = picked[0] * picked[1]
            pair[:, pl.ds(base, CHUNK)] = picked[1] * picked[2]
            pair[:, pl.ds(base + CHUNK, CHUNK)] = picked[0] * picked[2]
            pair[:, pl.ds(base + 2 * CHUNK, CHUNK)] = first
            partial = jnp.sum(first * picked[2], axis=0, keepdims=True)
            for i in range(CHUNK // LANES):
                ans[h, me_r, pl.ds(c * (CHUNK // LANES) + i, 1), :] = partial[:, i * LANES : (i + 1) * LANES]
            return carry

        lax.fori_loop(0, chunks, forward, 0)
        if h == 0:
            pl.semaphore_wait(barrier, n_row - 1 + n_z)
        for d in range(1, n_row):
            ans_copy(h, lax.rem(me_r + d, n_row), me_r, d).start()

    answer_scale = float(VALS**3) / total_rows
    half_lines = half_q // LANES

    def rows_at(block):
        return pl.ds(pl.multiple_of(block * BLOCK, BLOCK), BLOCK)

    def sums(block, h):
        span = slice(h * 3 * half_q, (h + 1) * 3 * half_q)
        return lax.dot_general(
            sel[rows_at(block), span], wgt[:, span], (((1,), (1,)), ((), ())),
            preferred_element_type=jnp.float32,
        )

    def piece(side, z):
        return pl.ds(pl.multiple_of(side * half_c + z * share, share), share)

    def sib_copy(side, z):
        return remote(acc.at[piece(side, z)], sib.at[z], sib_send.at[z], sib_recv.at[z], sibling)

    def z_copy(dst_z, slot):
        return remote(
            acc.at[piece(core, dst_z)], zin.at[slot], z_send.at[dst_z], z_recv.at[slot], (me_r, dst_z * 2 + core)
        )

    lower = me_z < n_z // 2

    def inner_at(b):
        return jnp.where(lower, n_block - 1 - b, b)

    def piece_at(b, i):
        return inner_at(b) * per_block + jnp.where(lower, per_block - 1 - i, i)

    for h in range(2):
        for d in range(1, n_row):
            ans_copy(h, me_r, lax.rem(me_r + n_row - d, n_row), d).wait_recv()
        total = ans[h, 0]
        for r in range(1, n_row):
            total = total + ans[h, r]
        lines = slice(h * half_lines, (h + 1) * half_lines)
        residual = total * answer_scale - tgt_ref[lines, :]
        res_ref[lines, :] = residual
        for line in range(half_lines):
            chunk, inner = divmod(line * LANES, CHUNK)
            for k in range(3):
                start = h * 3 * half_q + (chunk * 3 + k) * CHUNK + inner
                span = slice(start, start + LANES)
                wgt[:, span] = (pair[:, span] * residual[line : line + 1, :]).astype(jnp.bfloat16)
        if h == 0:
            span = slice(0, 3 * half_q)
            acc[...] = lax.dot_general(
                sel[:, span], wgt[:, span], (((1,), (1,)), ((), ())), preferred_element_type=jnp.float32
            )
    for b in range(n_block):
        block = other * n_block + inner_at(b)
        acc[rows_at(block), :] += sums(block, 1)
        for i in range(per_block):
            sib_copy(other, piece_at(b, i)).start()
    for b in range(n_block):
        block = core * n_block + inner_at(b)
        acc[rows_at(block), :] += sums(block, 1)
        for i in range(per_block):
            z = piece_at(b, i)
            sib_copy(core, z).wait_recv()
            summed = acc[piece(core, z), :] + sib[z]

            @pl.when(z != me_z)
            def _():
                acc[piece(core, z), :] = summed
                z_copy(z, me_z).start()

            @pl.when(z == me_z)
            def _():
                zin[me_z] = summed

    mine = piece(core, me_z)
    logit_share, relaxed_share = log_t[mine, :], rel_t[mine, :]
    for d in range(1, n_z):
        z_copy(me_z, lax.rem(me_z + d, n_z)).wait_recv()
    accumulated = zin[0]
    for z in range(1, n_z):
        accumulated = accumulated + zin[z]
    grouped_d = (float(VALS * VALS) * accumulated).reshape(share // VALS, VALS, rows)
    grouped_p = relaxed_share.reshape(share // VALS, VALS, rows)
    weighted_mean = jnp.sum(grouped_p * grouped_d, axis=1, keepdims=True)
    tangent = (grouped_p * (grouped_d - weighted_mean)).reshape(share, rows)
    gat[mine, :] = group_softmax(logit_share - STEP_RATE * tangent)

    def toward(d):
        sign = jnp.where(me_z < n_z // 2, 1, n_z - 1)
        return lax.rem(me_z + sign * d, n_z)

    def ag_copy(dst_z, z):
        return remote(
            gat.at[piece(core, z)], gat.at[piece(core, z)], ag_send.at[dst_z], ag_recv.at[z], (me_r, dst_z * 2 + core)
        )

    def fw_copy(side, z):
        return remote(gat.at[piece(side, z)], gat.at[piece(side, z)], fw_send.at[z], fw_recv.at[z], sibling)

    for d in range(n_z - 1, 0, -1):
        ag_copy(toward(d), me_z).start()
    fw_copy(core, me_z).start()
    for d in range(1, n_z):
        z = toward(d)
        ag_copy(z, z).wait_recv()
        fw_copy(core, z).start()
    for d in range(n_z):
        fw_copy(other, toward(d)).wait_recv()
    for h in range(2):
        for d in range(1, n_row):
            ans_copy(h, lax.rem(me_r + d, n_row), me_r, d).wait_send()
    for z in range(n_z):
        sib_copy(other, z).wait_send()
    for d in range(1, n_z):
        z = lax.rem(me_z + d, n_z)
        z_copy(z, me_z).wait_send()
        ag_copy(z, me_z).wait_send()
    for z in range(n_z):
        fw_copy(core, z).wait_send()


def finish(tall_ref, misfit_ref, new_ref, res_ref):
    for b in range(tall_ref.shape[0] // LANES):
        part = slice(b * LANES, (b + 1) * LANES)
        new_ref[:, part] = tall_ref[part, :].T
    res_ref[...] = misfit_ref[...]


def local(n_row, n_query, logits, attributes, values, targets):
    rows, cols = logits.shape
    queries = attributes.shape[1]
    n_z = n_query // 2
    share = cols // n_query
    dma = pltpu.SemaphoreType.DMA
    vmem = pl.BlockSpec(memory_space=pltpu.VMEM)
    columns = (attributes * VALS + values).astype(jnp.float32)
    meta = jnp.concatenate([columns, targets[None, :]], axis=0)
    tall, misfit = pl.pallas_call(
        functools.partial(kernel, n_row, n_query, rows * n_row),
        out_shape=(
            jax.ShapeDtypeStruct((cols, rows), jnp.float32),
            jax.ShapeDtypeStruct((queries // LANES, LANES), jnp.float32),
        ),
        in_specs=[vmem] * 2,
        out_specs=(vmem, vmem),
        scratch_shapes=[
            pltpu.VMEM((queries // LANES, LANES), jnp.float32),
            pltpu.VMEM((cols, rows), jnp.float32),
            pltpu.VMEM((cols, rows), jnp.float32),
            pltpu.VMEM((rows, cols), jnp.bfloat16),
            pltpu.VMEM((cols, 3 * queries), jnp.bfloat16),
            pltpu.VMEM((rows, 3 * queries), jnp.float32),
            pltpu.VMEM((rows, 3 * queries), jnp.bfloat16),
            pltpu.VMEM((2, n_row, queries // 2 // LANES, LANES), jnp.float32),
            pltpu.VMEM((cols, rows), jnp.float32),
            pltpu.VMEM((n_z, share, rows), jnp.float32),
            pltpu.VMEM((n_z, share, rows), jnp.float32),
            dma((2, n_row)), dma((2, n_row)),
            dma((n_z,)), dma((n_z,)), dma((n_z,)), dma((n_z,)),
            dma((n_z,)), dma((n_z,)), dma((n_z,)), dma((n_z,)),
        ],
        compiler_params=pltpu.CompilerParams(
            collective_id=0, has_side_effects=True, vmem_limit_bytes=48 * 1024 * 1024
        ),
    )(logits, meta)
    new_rows, residual = pl.pallas_call(
        finish,
        out_shape=(
            jax.ShapeDtypeStruct((rows, cols), jnp.float32),
            jax.ShapeDtypeStruct((queries // LANES, LANES), jnp.float32),
        ),
        in_specs=[vmem, vmem],
        out_specs=(vmem, vmem),
        compiler_params=pltpu.CompilerParams(vmem_limit_bytes=4 * 1024 * 1024),
    )(tall, misfit)
    return new_rows, residual.reshape(queries)


def solution(mesh):
    placed = (P("row", None), P(None, "query"), P(None, "query"), P("query"))
    return jax.shard_map(
        functools.partial(local, mesh.shape["row"], mesh.shape["query"]),
        mesh=mesh, in_specs=placed, out_specs=(P("row", None), P("query")), check_vma=False,
    )
```
